512 devices in a mesh: seq: 128 (over z, y, core), head: 4 (over x).
Axes of the slice: x: 4, y: 8, z: 8, core: 2. Of those that a mesh axis runs over, the one named last changes fastest.
Arguments:
- features: bfloat16 [16384, 1024], P('seq'), may hold values from -6 to 6
- w_in: bfloat16 [1024, 1024], P(None, 'head'), may hold values from -0.1875 to 0.1875
- b_ahead: bfloat16 [16384, 128], P('seq'), may hold values from -6 to 6
- c_ahead: bfloat16 [16384, 128], P('seq'), may hold values from -0.015625 to 0.015625
- b_behind: bfloat16 [16384, 128], P('seq'), may hold values from -6 to 6
- c_behind: bfloat16 [16384, 128], P('seq'), may hold values from -0.015625 to 0.015625
- decay_ahead: float32 [16, 16384], P('head', 'seq'), may hold values from -2 to 0, as said below
- decay_behind: float32 [16, 16384], P('head', 'seq'), may hold values from -2 to 0, as said below
- skip_gain: float32 [16], P('head'), may hold values from 0.5 to 1.5
- grad_y: bfloat16 [16384, 1024], P('seq', 'head'), may hold values from -6 to 6
Outputs:
- grad_features: bfloat16 [16384, 1024], P('seq', 'head')
- grad_w_in: float32 [1024, 1024], P('seq', 'head')
- grad_b_ahead: float32 [16384, 128], P('seq')
- grad_c_ahead: float32 [16384, 128], P('seq')
- grad_b_behind: float32 [16384, 128], P('seq')
- grad_c_behind: float32 [16384, 128], P('seq')
- grad_decay_ahead: float32 [16, 16384], P('head', 'seq')
- grad_decay_behind: float32 [16, 16384], P('head', 'seq')
The draws below stay inside these ranges and needn't reach their ends.
Inputs may be any that keep to these rules, and one draw needn't show every extreme that they name: `decay_ahead`: every log-decay is negative. `decay_behind`: every log-decay is negative.
All inputs are finite; a program needn't handle non-finite values.
Results may differ from the reference program's by a relative error of at most 0.039.
Values may be sent and summed in bfloat16 or wider, within the bound.
A program may use at most 128 MiB of HBM per device.

```python
import math
import jax
import jax.numpy as jnp
from jax import lax

D = 1024
ATTENTION_UNITS = 16
P_SIZE = 64
N = 128
SPAN = 128
T_DEV = 128
TOTAL_SLICES = 16384


def decay_table(key):
    keys = jax.random.split(key, 6)
    quick = jax.random.randint(keys[0], (ATTENTION_UNITS, 1), 0, 2) == 0
    starting_level = jnp.where(quick, 6.0 / SPAN, 0.7 / TOTAL_SLICES)
    starting_level = starting_level * jnp.exp(jax.random.uniform(keys[1], (ATTENTION_UNITS, 1), jnp.float32, -0.35, 0.35))
    blocks = TOTAL_SLICES // T_DEV
    multiplier_coefficient = jnp.exp(jax.random.uniform(keys[2], (1, blocks), jnp.float32, -0.357, 0.336))
    multiplier_coefficient = jnp.repeat(multiplier_coefficient, T_DEV, axis=1)
    approximate_guess = jax.random.uniform(keys[3], (ATTENTION_UNITS, TOTAL_SLICES), jnp.float32, 0.5, 1.5)
    selected_locations = jax.random.randint(keys[4], (3, ATTENTION_UNITS), 0, TOTAL_SLICES)
    increment_sizes = jax.random.uniform(keys[5], (3, ATTENTION_UNITS), jnp.float32, 0.22, 0.69)
    temporal_offset = jax.lax.broadcasted_iota(jnp.int32, (ATTENTION_UNITS, TOTAL_SLICES), 1)
    spike_clusters = jnp.zeros((ATTENTION_UNITS, TOTAL_SLICES), jnp.float32)
    for option_selector in range(3):
        spike_clusters = spike_clusters + jnp.where(temporal_offset == selected_locations[option_selector][:, None], increment_sizes[option_selector][:, None], 0.0)
    return -(starting_level * multiplier_coefficient * approximate_guess + spike_clusters)


def draw_decay_ahead(key, part):
    return decay_table(jax.random.fold_in(key, 11))


def draw_decay_behind(key, part):
    return decay_table(jax.random.fold_in(key, 23))


def level_of(key, shape, shards, low, largest):
    loudness = 1.0
    for position, blocks in shards:
        heights = jax.random.uniform(jax.random.fold_in(jax.random.fold_in(key, 6), position), (blocks,), jnp.float32, low / len(shards), largest / len(shards))
        loudness = loudness * jnp.repeat(jnp.exp(heights), shape[position] // blocks).reshape((-1,) + (1,) * (len(shape) - 1 - position))
    return loudness


def normal_values(key, shape, scale, reach, pieces=(), held_as=jnp.bfloat16):
    gain = level_of(key, shape, pieces, -0.22, 0.18) if pieces else 1.0
    values = jax.random.normal(key, shape, jnp.float32) * scale * gain
    return jnp.minimum(jnp.maximum(values, -reach), reach).astype(held_as)


def setup_inputs(seed: int = 0) -> dict:
    key_list = jax.random.split(jax.random.key(seed), 11)
    return {
        "features": normal_values(key_list[0], (TOTAL_SLICES, D), 1.0, 6.0, ((0, 128),)),
        "w_in": normal_values(key_list[1], (D, ATTENTION_UNITS * P_SIZE), D ** -0.5, 0.1875, ((1, 4),)),
        "b_ahead": normal_values(key_list[2], (TOTAL_SLICES, N), 1.0, 6.0, ((0, 128),)),
        "c_ahead": normal_values(key_list[3], (TOTAL_SLICES, N), (N * 8 * SPAN) ** -0.5, 0.015625, ((0, 128),)),
        "b_behind": normal_values(key_list[4], (TOTAL_SLICES, N), 1.0, 6.0, ((0, 128),)),
        "c_behind": normal_values(key_list[5], (TOTAL_SLICES, N), (N * 8 * SPAN) ** -0.5, 0.015625, ((0, 128),)),
        "decay_ahead": draw_decay_ahead(jax.random.fold_in(key_list[10], 71), 0),
        "decay_behind": draw_decay_behind(jax.random.fold_in(key_list[10], 71), 0),
        "skip_gain": jnp.clip(0.5 + 1.0 * jax.random.uniform(key_list[8], (ATTENTION_UNITS,), jnp.float32) ** level_of(key_list[8], (ATTENTION_UNITS,), ((0, 4),), -0.2, 0.2), 0.5, 1.5),
        "grad_y": normal_values(key_list[9], (TOTAL_SLICES, ATTENTION_UNITS * P_SIZE), 1.0, 6.0, ((0, 128), (1, 4))),
    }


HIGH = lax.Precision.HIGHEST

def block_step(states, inputs):
    signal, b_proj, c_proj, log_decay = inputs
    length = log_decay.shape[1]
    signal_low = signal.astype(jnp.bfloat16)
    b_low = b_proj.astype(jnp.bfloat16)
    c_low = c_proj.astype(jnp.bfloat16)
    cumulative = jnp.cumsum(log_decay, axis=1)
    row_index = lax.broadcasted_iota(jnp.int32, (length, length), 0)
    col_index = lax.broadcasted_iota(jnp.int32, (length, length), 1)
    causal = (col_index <= row_index)[None]
    spread = cumulative[:, :, None] - cumulative[:, None, :]
    decays = jnp.where(causal, jnp.exp(jnp.where(causal, spread, 0.0)), 0.0)
    affinity = jnp.dot(c_low, b_low.T, preferred_element_type=jnp.float32)
    scores = (decays * affinity[None]).astype(jnp.bfloat16)
    within = jnp.einsum('hts,shp->thp', scores, signal_low, preferred_element_type=jnp.float32)
    carried = jnp.exp(cumulative).T[:, :, None] * jnp.einsum('tn,hpn->thp', c_proj, states, precision=HIGH)
    final_log = cumulative[:, -1:]
    weighted = (signal * jnp.exp(final_log - cumulative).T[:, :, None]).astype(jnp.bfloat16)
    fresh = jnp.einsum('shp,sn->hpn', weighted, b_low, preferred_element_type=jnp.float32)
    return (jnp.exp(final_log)[:, :, None] * states + fresh, within + carried)

def scan_direction(signal, b_proj, c_proj, log_decay):
    length = SPAN
    blocks = signal.shape[0] // length
    heads = signal.shape[1]
    signal_blocks = signal.reshape(blocks, length, heads, signal.shape[2])
    b_blocks = b_proj.reshape(blocks, length, b_proj.shape[1])
    c_blocks = c_proj.reshape(blocks, length, c_proj.shape[1])
    decay_blocks = log_decay.reshape(heads, blocks, length).transpose(1, 0, 2)
    init = jnp.zeros((heads, signal.shape[2], b_proj.shape[1]), jnp.float32)
    _, outputs = lax.scan(jax.checkpoint(block_step), init, (signal_blocks, b_blocks, c_blocks, decay_blocks))
    return outputs.reshape(signal.shape)

def layer_core(signal, b_fore, c_fore, b_back, c_back, decay_fore, decay_back):
    ahead = scan_direction(signal, b_fore, c_fore, decay_fore)
    behind = scan_direction(jnp.flip(signal, 0), jnp.flip(b_back, 0), jnp.flip(c_back, 0), jnp.flip(decay_back, 1))
    return ahead + jnp.flip(behind, 0)

def reference(features, w_in, b_ahead, c_ahead, b_behind, c_behind, decay_ahead, decay_behind, skip_gain, grad_y):
    x_proj = jnp.dot(features, w_in, preferred_element_type=jnp.float32).astype(jnp.bfloat16)
    signal = x_proj.astype(jnp.float32).reshape(TOTAL_SLICES, ATTENTION_UNITS, P_SIZE)
    cotangent = grad_y.astype(jnp.float32).reshape(TOTAL_SLICES, ATTENTION_UNITS, P_SIZE)
    _, pullback = jax.vjp(layer_core, signal, b_ahead.astype(jnp.float32), c_ahead.astype(jnp.float32), b_behind.astype(jnp.float32), c_behind.astype(jnp.float32), decay_ahead, decay_behind)
    grad_sig, gb_fore, gc_fore, gb_back, gc_back, gd_fore, gd_back = pullback(cotangent)
    grad_x = (grad_sig + skip_gain[None, :, None] * cotangent).astype(jnp.bfloat16).reshape(TOTAL_SLICES, ATTENTION_UNITS * P_SIZE)
    grad_features = jnp.dot(grad_x, w_in.T, preferred_element_type=jnp.float32).astype(jnp.bfloat16)
    grad_w_in = jnp.dot(features.T, grad_x, preferred_element_type=jnp.float32) * (1.0 / math.sqrt(TOTAL_SLICES))
    return (grad_features, grad_w_in, gb_fore, gc_fore, gb_back, gc_back, gd_fore, gd_back)
```

```python
import math

import jax
import jax.numpy as jnp
from jax import lax
from jax.sharding import PartitionSpec as P

HIGH = lax.Precision.HIGHEST
BF = jnp.bfloat16
F32 = jnp.float32


def dot(a, b, dims, precision=None):
    return lax.dot_general(a, b, dims, precision=precision, preferred_element_type=F32)


def triangle(n, lower):
    row = lax.broadcasted_iota(jnp.int32, (n, n), 0)
    col = lax.broadcasted_iota(jnp.int32, (n, n), 1)
    return (col <= row) if lower else (col >= row)


def running(d, lower):
    mask = triangle(d.shape[1], lower).astype(F32)
    return dot(d, mask, (((1,), (1,)), ((), ())), HIGH)


def three(v):
    high = v.astype(BF)
    rest = v - high.astype(F32)
    mid = rest.astype(BF)
    low = (rest - mid.astype(F32)).astype(BF)
    return [high, mid, low]


def chain(gain, lower):
    n = gain.shape[0]
    row = lax.broadcasted_iota(jnp.int32, (n, n), 0)
    col = lax.broadcasted_iota(jnp.int32, (n, n), 1)
    before = (col < row) if lower else (col > row)
    terms = jnp.where(before, gain[:, None], 0.0)
    strict = before.astype(F32)
    total = dot(strict, terms, (((1,), (0,)), ((), ())), HIGH)
    return jnp.where(before, jnp.exp(total), 0.0)


def edge(k, lower):
    return k[:, -1:] if lower else k[:, :1]


def summaries(x, g, b, c, k, lower):
    final = edge(k, lower)
    weight = jnp.exp(final - k)
    weighted = (x.astype(F32) * weight[:, :, None]).astype(BF)
    fresh = jnp.einsum("hsp,sn->hpn", weighted, b, preferred_element_type=F32)
    grown = (g.astype(F32) * jnp.exp(k)[:, :, None]).astype(BF)
    back = jnp.einsum("htp,tn->hpn", grown, c, preferred_element_type=F32)
    return weighted, weight, grown, fresh, back


def gradients(x, g, b, c, k, weighted, weight, grown, dscores, s_in, g_out, lower):
    n = k.shape[1]
    mask = triangle(n, lower)[None]
    spread = k[:, :, None] - k[:, None, :]
    decays = jnp.where(mask, jnp.exp(jnp.where(mask, spread, 0.0)), 0.0)
    aff = dot(c, b, (((1,), (1,)), ((), ())))
    scores32 = decays * aff[None]
    scores = scores32.astype(BF)
    grad_x = jnp.einsum("hts,htp->hsp", scores, g, preferred_element_type=F32)
    e = dscores * scores32
    daff = jnp.sum(dscores * decays, axis=0).astype(BF)
    grad_c = dot(daff, b, (((1,), (0,)), ((), ())))
    grad_b = dot(daff, c, (((0,), (0,)), ((), ())))
    dk = jnp.sum(e, axis=2) - jnp.sum(e, axis=1)
    dweighted = jnp.einsum("sn,hpn->hsp", b, g_out, preferred_element_type=F32)
    scaled = dweighted * weight[:, :, None]
    grad_x = grad_x + scaled
    u = jnp.sum(scaled * x.astype(F32), axis=2)
    grad_b = grad_b + jnp.einsum("hsp,hpn->sn", weighted, g_out, preferred_element_type=F32)
    grad_c = grad_c + jnp.einsum("htp,hpn->tn", grown, s_in, preferred_element_type=F32)
    carried = jnp.einsum("tn,hpn->htp", c, s_in, preferred_element_type=F32)
    dk = dk - u + jnp.exp(k) * jnp.sum(carried * g.astype(F32), axis=2)
    final = edge(k, lower)
    both = jnp.sum(g_out.astype(F32) * s_in.astype(F32), axis=(1, 2))[:, None]
    last = jnp.sum(u, axis=1, keepdims=True) + jnp.exp(final) * both
    grad_d = dot(dk, triangle(n, lower).astype(F32), (((1,), (0,)), ((), ())), HIGH) + last
    return grad_x, grad_b, grad_c, grad_d


def local(features, w_in, b_a, c_a, b_z, c_z, decay_a, decay_z, skip_gain, grad_y):
    frames = features.shape[0]
    heads = decay_a.shape[0]
    size = w_in.shape[1] // heads
    peers = lax.axis_size("seq")
    n = b_a.shape[1]
    x2 = jnp.dot(features, w_in, preferred_element_type=F32).astype(BF)
    x = x2.reshape(frames, heads, size).transpose(1, 0, 2)
    g = grad_y.reshape(frames, heads, size).transpose(1, 0, 2)
    k_a = running(decay_a, True)
    k_z = running(decay_z, False)
    wt_a, w_a, gr_a, f_a, q_a = summaries(x, g, b_a, c_a, k_a, True)
    wt_z, w_z, gr_z, f_z, q_z = summaries(x, g, b_z, c_z, k_z, False)
    per = heads * size // peers
    parts = [v.astype(BF).reshape(peers, per * n) for v in (f_a, q_a, f_z, q_z)]
    gains = three(jnp.sum(decay_a, axis=1)) + three(jnp.sum(decay_z, axis=1))
    gains = jnp.repeat(jnp.stack(gains, 1), peers // heads, axis=0)
    gains = jnp.pad(gains, ((0, 0), (0, n - gains.shape[1])))
    sent = jnp.concatenate(parts + [gains], axis=1)
    got = lax.all_to_all(sent, "seq", 0, 0, tiled=True)
    wide = per * n
    gain = got[:, 4 * wide :].astype(F32)
    t_a = chain(gain[:, 0] + gain[:, 1] + gain[:, 2], True)
    t_z = chain(gain[:, 3] + gain[:, 4] + gain[:, 5], False)
    got = got[:, : 4 * wide].astype(F32)
    plain = (((1,), (0,)), ((), ()))
    flip = (((0,), (0,)), ((), ()))
    back = [
        dot(t_a, got[:, :wide], plain, HIGH),
        dot(t_a, got[:, wide : 2 * wide], flip, HIGH),
        dot(t_z, got[:, 2 * wide : 3 * wide], plain, HIGH),
        dot(t_z, got[:, 3 * wide :], flip, HIGH),
    ]
    back = jnp.concatenate(back, axis=1).astype(BF)
    back = lax.all_to_all(back, "seq", 0, 0, tiled=True)
    s_a, o_a, s_z, o_z = [
        back[:, i * wide : (i + 1) * wide].reshape(heads, size, n) for i in range(4)
    ]
    dscores = jnp.einsum("htp,hsp->hts", g, x, preferred_element_type=F32).astype(BF).astype(F32)
    gx_a, gb_a, gc_a, gd_a = gradients(x, g, b_a, c_a, k_a, wt_a, w_a, gr_a, dscores, s_a, o_a, True)
    gx_z, gb_z, gc_z, gd_z = gradients(x, g, b_z, c_z, k_z, wt_z, w_z, gr_z, dscores, s_z, o_z, False)
    grad_x = gx_a + gx_z + skip_gain[:, None, None] * g.astype(F32)
    grad_x = grad_x.astype(BF).transpose(1, 0, 2).reshape(frames, heads * size)
    maps = jnp.concatenate([gb_a, gc_a, gb_z, gc_z], axis=1).astype(BF)
    maps = lax.psum(maps, "head").astype(F32)
    terms = dot(grad_x, w_in, (((1,), (1,)), ((), ()))).astype(BF)
    grad_features = lax.psum_scatter(terms, "head", scatter_dimension=1, tiled=True)
    weight_sum = lax.psum_scatter(
        dot(features, grad_x, flip), "seq", scatter_dimension=0, tiled=True
    )
    grad_w_in = weight_sum * (1.0 / math.sqrt(frames * peers))
    return (
        grad_features,
        grad_w_in,
        maps[:, :n],
        maps[:, n : 2 * n],
        maps[:, 2 * n : 3 * n],
        maps[:, 3 * n :],
        gd_a,
        gd_z,
    )


def solution(mesh):
    in_specs = (
        P("seq", None),
        P(None, "head"),
        P("seq", None),
        P("seq", None),
        P("seq", None),
        P("seq", None),
        P("head", "seq"),
        P("head", "seq"),
        P("head"),
        P("seq", "head"),
    )
    out_specs = (
        P("seq", "head"),
        P("seq", "head"),
        P("seq", None),
        P("seq", None),
        P("seq", None),
        P("seq", None),
        P("head", "seq"),
        P("head", "seq"),
    )
    return jax.shard_map(local, mesh=mesh, in_specs=in_specs, out_specs=out_specs, check_vma=False)
```

```python
import functools
import math

import jax
import jax.numpy as jnp
from jax import lax
from jax.experimental import pallas as pl
from jax.experimental.pallas import tpu as pltpu
from jax.sharding import PartitionSpec as P

HIGH = lax.Precision.HIGHEST
BF = jnp.bfloat16
F32 = jnp.float32
Y = 8
C = 2
G = Y * C
MESH = pl.DeviceIdType.MESH


def dot(a, b, dims, precision=None):
    return lax.dot_general(a, b, dims, precision=precision, preferred_element_type=F32)


def triangle(n, lower):
    row = lax.broadcasted_iota(jnp.int32, (n, n), 0)
    col = lax.broadcasted_iota(jnp.int32, (n, n), 1)
    return (col <= row) if lower else (col >= row)


def running(d, lower):
    mask = triangle(d.shape[1], lower).astype(F32)
    return dot(d, mask, (((1,), (1,)), ((), ())), HIGH)


def greet(peers):
    barrier = pltpu.get_barrier_semaphore()
    for axis, first, count, step, me in peers:

        def signal(k, carry):
            peer = first + lax.rem(me + k, count) * step
            pl.semaphore_signal(barrier, inc=1, device_id={axis: peer}, device_id_type=MESH)
            return carry

        lax.fori_loop(1, count, signal, 0)
    pl.semaphore_wait(barrier, sum(p[2] - 1 for p in peers))


def spread_out(group, source, target, send_sem, recv_sem):
    axis, first, count, step, me = group
    pltpu.make_async_copy(source(me), target(me), recv_sem).start()

    def send(k, carry):
        peer = lax.rem(me + k, count)
        pltpu.make_async_remote_copy(
            src_ref=source(peer),
            dst_ref=target(me),
            send_sem=send_sem,
            recv_sem=recv_sem,
            device_id={axis: first + peer * step},
            device_id_type=MESH,
        ).start()
        return carry

    lax.fori_loop(1, count, send, 0)


def take(ref, sem):
    pltpu.make_async_copy(ref, ref, sem).wait()


def carry_kernel(zs, f_ref, gain_ref, out_ref, held, gains, total, tgain, zheld, zgains, back, sems):
    seq = lax.axis_index("seq")
    z, r = seq // G, lax.rem(seq, G)
    near = ("seq", z * G, G, 1, r)
    far = ("seq", r, zs, G, z)
    greet([near, far])
    spread_out(near, lambda k: gain_ref, lambda k: gains.at[k], sems.at[0], sems.at[1])
    spread_out(near, lambda k: f_ref.at[k], lambda k: held.at[k], sems.at[2], sems.at[3])
    head = r // (G // 4)
    take(gains, sems.at[1])
    take(held, sems.at[3])
    ups = (True, False, False, True)

    def grow(ref, j, i):
        return jnp.exp(ref[j, pl.ds((i // 2) * 4 + head, 1), :])

    for i, up in enumerate(ups):
        state = jnp.zeros(total.shape[1:], F32)
        for j in range(G) if up else range(G - 1, -1, -1):
            state = grow(gains, j, i) * state + held[j, i].astype(F32)
        total[i] = state.astype(BF)
    whole = gains[0]
    for j in range(1, G):
        whole = whole + gains[j]
    tgain[...] = whole
    spread_out(far, lambda k: tgain, lambda k: zgains.at[k], sems.at[4], sems.at[5])
    spread_out(far, lambda k: total, lambda k: zheld.at[k], sems.at[6], sems.at[7])
    take(zgains, sems.at[5])
    take(zheld, sems.at[7])
    for i, up in enumerate(ups):
        state = jnp.zeros(total.shape[1:], F32)
        for j in range(zs) if up else range(zs - 1, -1, -1):
            new = grow(zgains, j, i) * state + zheld[j, i].astype(F32)
            state = jnp.where((j < z) if up else (j > z), new, state)
        for j in range(G) if up else range(G - 1, -1, -1):
            back[j, i] = state.astype(BF)
            state = grow(gains, j, i) * state + held[j, i].astype(F32)
    spread_out(near, lambda k: back.at[k], lambda k: out_ref.at[k], sems.at[8], sems.at[9])
    take(out_ref, sems.at[9])
    few = G - 1
    take(gains.at[pl.ds(0, few)], sems.at[0])
    take(held.at[pl.ds(0, few)], sems.at[2])
    take(zgains.at[pl.ds(0, zs - 1)], sems.at[4])
    take(zheld.at[pl.ds(0, zs - 1)], sems.at[6])
    take(back.at[pl.ds(0, few)], sems.at[8])


def carry_states(f, gain, zs):
    vmem = pl.BlockSpec(memory_space=pltpu.VMEM)
    part = f.shape[1:]
    return pl.pallas_call(
        functools.partial(carry_kernel, zs),
        out_shape=jax.ShapeDtypeStruct(f.shape, BF),
        in_specs=[vmem, vmem],
        out_specs=vmem,
        scratch_shapes=[
            pltpu.VMEM(f.shape, BF),
            pltpu.VMEM((G,) + gain.shape, F32),
            pltpu.VMEM(part, BF),
            pltpu.VMEM(gain.shape, F32),
            pltpu.VMEM((zs,) + part, BF),
            pltpu.VMEM((zs,) + gain.shape, F32),
            pltpu.VMEM(f.shape, BF),
            pltpu.SemaphoreType.DMA((10,)),
        ],
        compiler_params=pltpu.CompilerParams(collective_id=0, has_side_effects=True),
    )(f, gain)


def tail_kernel(
    zs, scale, w_ref, m_ref, f_ref, gf_ref, gw_ref, gm_ref,
    w_core, w_mid, w_y, w_low, w_z, m_all, f_all, sems,
):
    seq = lax.axis_index("seq")
    hd = lax.axis_index("head")
    z, r = seq // G, lax.rem(seq, G)
    y, core = r // C, lax.rem(r, C)
    heads = m_all.shape[0]
    along_c = ("seq", z * G + y * C, C, 1, core)
    along_y = ("seq", z * G + core, Y, C, y)
    along_z = ("seq", r, zs, G, z)
    along_x = ("head", 0, heads, 1, hd)
    greet([along_c, along_y, along_z, along_x])
    spread_out(along_c, lambda k: w_ref.at[:, :, k], lambda k: w_core.at[k], sems.at[0], sems.at[1])
    spread_out(along_x, lambda k: f_ref.at[k], lambda k: f_all.at[k], sems.at[2], sems.at[3])
    spread_out(along_x, lambda k: m_ref, lambda k: m_all.at[k], sems.at[4], sems.at[5])
    take(w_core, sems.at[1])
    for j in range(Y):
        w_mid[j] = (w_core[0, :, j].astype(F32) + w_core[1, :, j].astype(F32)).astype(BF)
    spread_out(along_y, lambda k: w_mid.at[k], lambda k: w_y.at[k], sems.at[6], sems.at[7])
    take(w_y, sems.at[7])
    for i in range(zs):
        low = w_y[0, i].astype(F32)
        for j in range(1, Y):
            low = low + w_y[j, i].astype(F32)
        w_low[i] = low.astype(BF)
    spread_out(along_z, lambda k: w_low.at[k], lambda k: w_z.at[k], sems.at[8], sems.at[9])
    take(f_all, sems.at[3])
    take(m_all, sems.at[5])
    f = f_all[0].astype(F32)
    for j in range(1, heads):
        f = f + f_all[j].astype(F32)
    gf_ref[...] = f.astype(BF)
    n = gm_ref.shape[2]
    for i in range(gm_ref.shape[0]):
        m = m_all[0, :, i * n : (i + 1) * n].astype(F32)
        for j in range(1, heads):
            m = m + m_all[j, :, i * n : (i + 1) * n].astype(F32)
        gm_ref[i] = m
    take(w_z, sems.at[9])
    low = w_z[0].astype(F32)
    for j in range(1, zs):
        low = low + w_z[j].astype(F32)
    gw_ref[...] = low * scale
    take(w_core.at[0], sems.at[0])
    take(f_all.at[pl.ds(0, heads - 1)], sems.at[2])
    take(m_all.at[pl.ds(0, heads - 1)], sems.at[4])
    take(w_y.at[pl.ds(0, Y - 1)], sems.at[6])
    take(w_z.at[pl.ds(0, zs - 1)], sems.at[8])


def tail(w, maps, terms, zs, scale):
    vmem = pl.BlockSpec(memory_space=pltpu.VMEM)
    heads, frames, width = terms.shape
    rows, cols = w.shape[3:]
    n = maps.shape[1] // 4
    return pl.pallas_call(
        functools.partial(tail_kernel, zs, scale),
        out_shape=[
            jax.ShapeDtypeStruct((frames, width), BF),
            jax.ShapeDtypeStruct((rows, cols), F32),
            jax.ShapeDtypeStruct((4, frames, n), F32),
        ],
        in_specs=[vmem] * 3,
        out_specs=[vmem] * 3,
        scratch_shapes=[
            pltpu.VMEM((C, zs, Y, rows, cols), BF),
            pltpu.VMEM((Y, zs, rows, cols), BF),
            pltpu.VMEM((Y, zs, rows, cols), BF),
            pltpu.VMEM((zs, rows, cols), BF),
            pltpu.VMEM((zs, rows, cols), BF),
            pltpu.VMEM((heads,) + maps.shape, BF),
            pltpu.VMEM(terms.shape, BF),
            pltpu.SemaphoreType.DMA((10,)),
        ],
        compiler_params=pltpu.CompilerParams(collective_id=1, has_side_effects=True),
    )(w, maps, terms)


def edge(k, lower):
    return k[:, -1:] if lower else k[:, :1]


def summaries(x, g, b, c, k, lower):
    final = edge(k, lower)
    weight = jnp.exp(final - k)
    weighted = (x.astype(F32) * weight[:, :, None]).astype(BF)
    fresh = jnp.einsum("hsp,sn->hpn", weighted, b, preferred_element_type=F32)
    grown = (g.astype(F32) * jnp.exp(k)[:, :, None]).astype(BF)
    back = jnp.einsum("htp,tn->hpn", grown, c, preferred_element_type=F32)
    return weighted, weight, grown, fresh, back


def gradients(x, g, b, c, k, weighted, weight, grown, dscores, s_in, g_out, lower):
    n = k.shape[1]
    mask = triangle(n, lower)[None]
    spread = k[:, :, None] - k[:, None, :]
    decays = jnp.where(mask, jnp.exp(jnp.where(mask, spread, 0.0)), 0.0)
    aff = dot(c, b, (((1,), (1,)), ((), ())))
    scores32 = decays * aff[None]
    scores = scores32.astype(BF)
    grad_x = jnp.einsum("hts,htp->hsp", scores, g, preferred_element_type=F32)
    e = dscores * scores32
    daff = jnp.sum(dscores * decays, axis=0).astype(BF)
    grad_c = dot(daff, b, (((1,), (0,)), ((), ())))
    grad_b = dot(daff, c, (((0,), (0,)), ((), ())))
    dk = jnp.sum(e, axis=2) - jnp.sum(e, axis=1)
    dweighted = jnp.einsum("sn,hpn->hsp", b, g_out, preferred_element_type=F32)
    scaled = dweighted * weight[:, :, None]
    grad_x = grad_x + scaled
    u = jnp.sum(scaled * x.astype(F32), axis=2)
    grad_b = grad_b + jnp.einsum("hsp,hpn->sn", weighted, g_out, preferred_element_type=F32)
    grad_c = grad_c + jnp.einsum("htp,hpn->tn", grown, s_in, preferred_element_type=F32)
    carried = jnp.einsum("tn,hpn->htp", c, s_in, preferred_element_type=F32)
    dk = dk - u + jnp.exp(k) * jnp.sum(carried * g.astype(F32), axis=2)
    final = edge(k, lower)
    both = jnp.sum(g_out.astype(F32) * s_in.astype(F32), axis=(1, 2))[:, None]
    last = jnp.sum(u, axis=1, keepdims=True) + jnp.exp(final) * both
    grad_d = dot(dk, triangle(n, lower).astype(F32), (((1,), (0,)), ((), ())), HIGH) + last
    return grad_x, grad_b, grad_c, grad_d


def local(features, w_in, b_a, c_a, b_z, c_z, decay_a, decay_z, skip_gain, grad_y):
    frames = features.shape[0]
    heads = decay_a.shape[0]
    size = w_in.shape[1] // heads
    peers = lax.axis_size("seq")
    heads_all = lax.axis_size("head")
    n = b_a.shape[1]
    x2 = jnp.dot(features, w_in, preferred_element_type=F32).astype(BF)
    x = x2.reshape(frames, heads, size).transpose(1, 0, 2)
    g = grad_y.reshape(frames, heads, size).transpose(1, 0, 2)
    k_a = running(decay_a, True)
    k_z = running(decay_z, False)
    wt_a, w_a, gr_a, f_a, q_a = summaries(x, g, b_a, c_a, k_a, True)
    wt_z, w_z, gr_z, f_z, q_z = summaries(x, g, b_z, c_z, k_z, False)
    rows = heads * size // G
    sent = jnp.stack([v.astype(BF).reshape(G, rows, n) for v in (f_a, q_a, f_z, q_z)], axis=1)
    gain = jnp.concatenate([jnp.sum(decay_a, axis=1), jnp.sum(decay_z, axis=1)])
    gain = jnp.broadcast_to(gain[:, None], (2 * heads, n))
    back = carry_states(sent, gain, peers // G)
    s_a, o_a, s_z, o_z = [back[:, i].reshape(heads, size, n) for i in range(4)]
    dscores = jnp.einsum("htp,hsp->hts", g, x, preferred_element_type=F32).astype(BF).astype(F32)
    gx_a, gb_a, gc_a, gd_a = gradients(x, g, b_a, c_a, k_a, wt_a, w_a, gr_a, dscores, s_a, o_a, True)
    gx_z, gb_z, gc_z, gd_z = gradients(x, g, b_z, c_z, k_z, wt_z, w_z, gr_z, dscores, s_z, o_z, False)
    grad_x = gx_a + gx_z + skip_gain[:, None, None] * g.astype(F32)
    grad_x = grad_x.astype(BF).transpose(1, 0, 2).reshape(frames, heads * size)
    maps = jnp.concatenate([gb_a, gc_a, gb_z, gc_z], axis=1).astype(BF)
    split = w_in.reshape(heads_all, -1, w_in.shape[1])
    terms = jnp.einsum("tk,hdk->htd", grad_x, split, preferred_element_type=F32).astype(BF)
    weight = dot(features, grad_x, (((0,), (0,)), ((), ()))).astype(BF)
    weight = weight.reshape(peers // G, Y, C, -1, weight.shape[1])
    grad_features, grad_w_in, maps = tail(
        weight, maps, terms, peers // G, 1.0 / math.sqrt(frames * peers)
    )
    return (grad_features, grad_w_in, maps[0], maps[1], maps[2], maps[3], gd_a, gd_z)


def solution(mesh):
    in_specs = (
        P("seq", None),
        P(None, "head"),
        P("seq", None),
        P("seq", None),
        P("seq", None),
        P("seq", None),
        P("head", "seq"),
        P("head", "seq"),
        P("head"),
        P("seq", "head"),
    )
    out_specs = (
        P("seq", "head"),
        P("seq", "head"),
        P("seq", None),
        P("seq", None),
        P("seq", None),
        P("seq", None),
        P("head", "seq"),
        P("head", "seq"),
    )
    return jax.shard_map(local, mesh=mesh, in_specs=in_specs, out_specs=out_specs, check_vma=False)
```

```python
import functools
import math

import jax
import jax.numpy as jnp
from jax import lax
from jax.experimental import pallas as pl
from jax.experimental.pallas import tpu as pltpu
from jax.sharding import PartitionSpec as P

HIGH = lax.Precision.HIGHEST
BF = jnp.bfloat16
F32 = jnp.float32
Y = 8
C = 2
G = Y * C
MESH = pl.DeviceIdType.MESH


def greet(peers):
    barrier = pltpu.get_barrier_semaphore()
    for axis, first, count, step, me in peers:

        def signal(k, carry):
            peer = first + lax.rem(me + k, count) * step
            pl.semaphore_signal(barrier, inc=1, device_id={axis: peer}, device_id_type=MESH)
            return carry

        lax.fori_loop(1, count, signal, 0)


def greeted(peers):
    pl.semaphore_wait(pltpu.get_barrier_semaphore(), sum(p[2] - 1 for p in peers))


def spread_out(group, source, target, send_sem, recv_sem):
    axis, first, count, step, me = group
    pltpu.make_async_copy(source(me), target(me), recv_sem).start()

    def send(k, carry):
        peer = lax.rem(me + k, count)
        pltpu.make_async_remote_copy(
            src_ref=source(peer),
            dst_ref=target(me),
            send_sem=send_sem,
            recv_sem=recv_sem,
            device_id={axis: first + peer * step},
            device_id_type=MESH,
        ).start()
        return carry

    lax.fori_loop(1, count, send, 0)


def take(ref, sem):
    pltpu.make_async_copy(ref, ref, sem).wait()


NN = (((1,), (0,)), ((), ()))
NT = (((1,), (1,)), ((), ()))
TN = (((0,), (0,)), ((), ()))
UPS = ((True, False), (False, True))


def dot(a, b, dims, precision=None):
    return lax.dot_general(a, b, dims, precision=precision, preferred_element_type=F32)


def iota(shape, axis):
    return lax.broadcasted_iota(jnp.int32, shape, axis)


def layer_kernel(
    zs, heads, scale,
    x_ref, w_ref, ba_ref, ca_ref, bz_ref, cz_ref, da_ref, dz_ref, skip_ref, g_ref,
    gf_ref, gw_ref, gba_ref, gca_ref, gbz_ref, gcz_ref, gda_ref, gdz_ref,
    d8, sent, held, gains, total, tgain, zheld, zgains, back, states, ds,
    w_all, w_core, w_mid, w_y, w_low, w_z, m_own, m_all, f_own, f_all, sems,
):
    seq = lax.axis_index("seq")
    hd = lax.axis_index("head")
    z, r = seq // G, lax.rem(seq, G)
    y, core = r // C, lax.rem(r, C)
    groups = f_all.shape[0]
    near = ("seq", z * G, G, 1, r)
    far = ("seq", r, zs, G, z)
    along_c = ("seq", z * G + y * C, C, 1, core)
    along_y = ("seq", z * G + core, Y, C, y)
    along_x = ("head", 0, groups, 1, hd)
    greet([near, far, along_x])

    frames, wide = g_ref.shape
    size = wide // heads
    n = ba_ref.shape[1]
    rows = wide // G
    low_mask = iota((frames, frames), 1) <= iota((frames, frames), 0)
    high_mask = iota((frames, frames), 1) >= iota((frames, frames), 0)
    low_f, high_f = low_mask.astype(F32), high_mask.astype(F32)
    which = iota((2 * heads, wide), 1) // size
    pick = [(iota((2 * heads, wide), 0) - i * heads == which).astype(F32) for i in range(2)]
    d8[0:heads, :] = da_ref[...]
    d8[heads : 2 * heads, :] = dz_ref[...]
    d = d8[...]
    tgain[0] = jnp.broadcast_to(jnp.sum(d, axis=1, keepdims=True), (2 * heads, n))
    k_row = [dot(d, low_f, NT, HIGH), dot(d, high_f, NT, HIGH)]
    k_all = [dot(k_row[i], pick[i], TN, HIGH) for i in range(2)]
    edge = [k_all[0][frames - 1 : frames], k_all[1][0:1]]
    weight = [jnp.exp(edge[i] - k_all[i]) for i in range(2)]
    growth = [jnp.exp(k_all[i]) for i in range(2)]
    g = g_ref[...]
    g32 = g.astype(F32)
    grown = [(g32 * growth[i]).astype(BF) for i in range(2)]
    maps_b = [ba_ref, bz_ref]
    maps_c = [ca_ref, cz_ref]
    x = dot(x_ref[...], w_ref[...], NN).astype(BF)
    x32 = x.astype(F32)
    weighted = [(x32 * weight[i]).astype(BF) for i in range(2)]
    greeted([near, far, along_x])
    spread_out(near, lambda k: tgain.at[0], lambda k: gains.at[k], sems.at[0], sems.at[1])
    for i in range(2):
        fresh = dot(weighted[i], maps_b[i][...], TN).astype(BF)
        query = dot(grown[i], maps_c[i][...], TN).astype(BF)
        sent[i, :, 0] = fresh.reshape(G, rows, n)
        sent[i, :, 1] = query.reshape(G, rows, n)
        spread_out(
            near, lambda k: sent.at[i, k], lambda k: held.at[i, k], sems.at[2 + i], sems.at[4 + i]
        )

    lane_head = iota((frames, wide), 1) // size
    grad_x = jnp.zeros((frames, wide), F32)
    dk = jnp.zeros((2 * heads, frames), F32)
    daff = [None, None]
    for i in range(2):
        mask = low_mask if i == 0 else high_mask
        aff = dot(maps_c[i][...], maps_b[i][...], NT)
        pull = jnp.zeros((frames, frames), F32)
        for h in range(heads):
            gm = jnp.where(lane_head == h, g32, 0.0).astype(BF)
            if i == 0:
                ds[h] = dot(gm, x, NT).astype(BF)
            dscores = ds[h].astype(F32)
            row = i * heads + h
            kc = k_all[i][:, h * size : h * size + 1]
            kr = k_row[i][row : row + 1]
            decays = jnp.where(mask, jnp.exp(jnp.where(mask, kc - kr, 0.0)), 0.0)
            scores = decays * aff
            grad_x = grad_x + dot(scores.astype(BF), gm, TN)
            pull = pull + dscores * decays
            e = dscores * scores
            mine = iota((2 * heads, frames), 0) == row
            dk = dk + dot(mine.astype(F32), e, NT, HIGH)
            dk = dk - jnp.where(mine, jnp.sum(e, axis=0, keepdims=True), 0.0)
        daff[i] = pull.astype(BF)
        if i == 0:
            take(gains, sems.at[1])
            head = r // (G // heads)

            def grow(ref, j, side):
                return jnp.exp(ref[j, pl.ds(side * heads + head, 1), :])

            whole = gains[0]
            for j in range(1, G):
                whole = whole + gains[j]
            tgain[1] = whole
            spread_out(far, lambda k: tgain.at[1], lambda k: zgains.at[k], sems.at[6], sems.at[7])
            for side in range(2):
                take(held.at[side], sems.at[4 + side])
                for j0, up in enumerate(UPS[side]):
                    state = jnp.zeros((rows, n), F32)
                    for j in range(G) if up else range(G - 1, -1, -1):
                        state = grow(gains, j, side) * state + held[side, j, j0].astype(F32)
                    total[side, j0] = state.astype(BF)
                spread_out(
                    far,
                    lambda k: total.at[side],
                    lambda k: zheld.at[side, k],
                    sems.at[8 + side],
                    sems.at[10 + side],
                )

    take(zgains, sems.at[7])
    for side in range(2):
        take(zheld.at[side], sems.at[10 + side])
        for j0, up in enumerate(UPS[side]):
            state = jnp.zeros((rows, n), F32)
            for j in range(zs) if up else range(zs - 1, -1, -1):
                new = grow(zgains, j, side) * state + zheld[side, j, j0].astype(F32)
                state = jnp.where((j < z) if up else (j > z), new, state)
            for j in range(G) if up else range(G - 1, -1, -1):
                back[side, j, j0] = state.astype(BF)
                state = grow(gains, j, side) * state + held[side, j, j0].astype(F32)
        spread_out(
            near,
            lambda k: back.at[side, k],
            lambda k: states.at[side, k],
            sems.at[12 + side],
            sems.at[14 + side],
        )
    grad_b = [dot(daff[i], maps_c[i][...], TN) for i in range(2)]
    grad_c = [dot(daff[i], maps_b[i][...], NN) for i in range(2)]
    lane = iota((1, wide), 1) // size
    skip = jnp.zeros((1, wide), F32)
    for h in range(heads):
        skip = jnp.where(lane == h, skip_ref[h], skip)
    grad_x = grad_x + skip * g32

    last = jnp.zeros((2 * heads, n), F32)
    for i in range(2):
        take(states.at[i], sems.at[14 + i])
        s_in = states[i, :, 0].reshape(wide, n)
        g_out = states[i, :, 1].reshape(wide, n)
        scaled = dot(maps_b[i][...], g_out, NT) * weight[i]
        grad_x = grad_x + scaled
        u = dot(pick[i], scaled * x32, NT, HIGH)
        carried = dot(maps_c[i][...], s_in, NT) * growth[i] * g32
        dk = dk - u + dot(pick[i], carried, NT, HIGH)
        both = dot(pick[i], g_out.astype(F32) * s_in.astype(F32), NN, HIGH)
        fall = jnp.exp(jnp.sum(d, axis=1, keepdims=True))
        last = last + u + fall * both
        m_own[:, (2 * i) * n : (2 * i + 1) * n] = (grad_b[i] + dot(weighted[i], g_out, NN)).astype(BF)
        m_own[:, (2 * i + 1) * n : (2 * i + 2) * n] = (grad_c[i] + dot(grown[i], s_in, NN)).astype(BF)
    gx = grad_x.astype(BF)
    piece = Y * C * w_all.shape[3]
    for k in range(zs):
        part = dot(x_ref[:, k * piece : (k + 1) * piece], gx, TN)
        w_all[k] = part.reshape(w_all.shape[1:]).astype(BF)
    spread_out(along_c, lambda k: w_all.at[:, :, k], lambda k: w_core.at[k], sems.at[16], sems.at[17])
    spread_out(along_x, lambda k: m_own, lambda k: m_all.at[k], sems.at[18], sems.at[19])
    for k in range(groups):
        f_own[k] = dot(gx, w_ref[k * wide : (k + 1) * wide, :], NT).astype(BF)
    spread_out(along_x, lambda k: f_own.at[k], lambda k: f_all.at[k], sems.at[20], sems.at[21])
    tri = jnp.where(iota((2 * heads, frames), 0) < heads, dot(dk, low_f, NN, HIGH), dot(dk, high_f, NN, HIGH))
    grad_d = tri + jnp.sum(last, axis=1, keepdims=True)
    gda_ref[...] = grad_d[0:heads]
    gdz_ref[...] = grad_d[heads : 2 * heads]
    take(w_core, sems.at[17])
    for j in range(Y):
        w_mid[j] = (w_core[0, :, j].astype(F32) + w_core[1, :, j].astype(F32)).astype(BF)
    spread_out(along_y, lambda k: w_mid.at[k], lambda k: w_y.at[k], sems.at[22], sems.at[23])
    take(w_y, sems.at[23])
    for i in range(zs):
        low = w_y[0, i].astype(F32)
        for j in range(1, Y):
            low = low + w_y[j, i].astype(F32)
        w_low[i] = low.astype(BF)
    spread_out(far, lambda k: w_low.at[k], lambda k: w_z.at[k], sems.at[24], sems.at[25])
    take(m_all, sems.at[19])
    for i, ref in enumerate((gba_ref, gca_ref, gbz_ref, gcz_ref)):
        m = m_all[0, :, i * n : (i + 1) * n].astype(F32)
        for j in range(1, groups):
            m = m + m_all[j, :, i * n : (i + 1) * n].astype(F32)
        ref[...] = m
    take(f_all, sems.at[21])
    f = f_all[0].astype(F32)
    for j in range(1, groups):
        f = f + f_all[j].astype(F32)
    gf_ref[...] = f.astype(BF)
    take(w_z, sems.at[25])
    low = w_z[0].astype(F32)
    for j in range(1, zs):
        low = low + w_z[j].astype(F32)
    gw_ref[...] = low * scale
    few, far_few, x_few = pl.ds(0, G - 1), pl.ds(0, zs - 1), pl.ds(0, groups - 1)
    take(gains.at[few], sems.at[0])
    take(zgains.at[far_few], sems.at[6])
    for i in range(2):
        take(held.at[i, few], sems.at[2 + i])
        take(zheld.at[i, far_few], sems.at[8 + i])
        take(back.at[i, few], sems.at[12 + i])
    take(w_core.at[0], sems.at[16])
    take(m_all.at[x_few], sems.at[18])
    take(f_all.at[x_few], sems.at[20])
    take(w_y.at[pl.ds(0, Y - 1)], sems.at[22])
    take(w_z.at[far_few], sems.at[24])


def local(*args):
    features, w_in, b_a, _, _, _, decay_a, _, _, grad_y = args
    frames, deep = features.shape
    heads = decay_a.shape[0]
    wide = w_in.shape[1]
    n = b_a.shape[1]
    zs = lax.axis_size("seq") // G
    groups = lax.axis_size("head")
    cut = deep // (zs * G)
    rows = wide // G
    vmem = pl.BlockSpec(memory_space=pltpu.VMEM)
    smem = pl.BlockSpec(memory_space=pltpu.SMEM)
    scale = 1.0 / math.sqrt(frames * zs * G)
    out = jax.ShapeDtypeStruct
    return pl.pallas_call(
        functools.partial(layer_kernel, zs, heads, scale),
        out_shape=[
            out((frames, deep // groups), BF),
            out((cut, wide), F32),
            out((frames, n), F32),
            out((frames, n), F32),
            out((frames, n), F32),
            out((frames, n), F32),
            out((heads, frames), F32),
            out((heads, frames), F32),
        ],
        in_specs=[vmem] * 8 + [smem, vmem],
        out_specs=[vmem] * 8,
        scratch_shapes=[
            pltpu.VMEM((2 * heads, frames), F32),
            pltpu.VMEM((2, G, 2, rows, n), BF),
            pltpu.VMEM((2, G, 2, rows, n), BF),
            pltpu.VMEM((G, 2 * heads, n), F32),
            pltpu.VMEM((2, 2, rows, n), BF),
            pltpu.VMEM((2, 2 * heads, n), F32),
            pltpu.VMEM((2, zs, 2, rows, n), BF),
            pltpu.VMEM((zs, 2 * heads, n), F32),
            pltpu.VMEM((2, G, 2, rows, n), BF),
            pltpu.VMEM((2, G, 2, rows, n), BF),
            pltpu.VMEM((heads, frames, frames), BF),
            pltpu.VMEM((zs, Y, C, cut, wide), BF),
            pltpu.VMEM((C, zs, Y, cut, wide), BF),
            pltpu.VMEM((Y, zs, cut, wide), BF),
            pltpu.VMEM((Y, zs, cut, wide), BF),
            pltpu.VMEM((zs, cut, wide), BF),
            pltpu.VMEM((zs, cut, wide), BF),
            pltpu.VMEM((frames, 4 * n), BF),
            pltpu.VMEM((groups, frames, 4 * n), BF),
            pltpu.VMEM((groups, frames, wide), BF),
            pltpu.VMEM((groups, frames, wide), BF),
            pltpu.SemaphoreType.DMA((26,)),
        ],
        compiler_params=pltpu.CompilerParams(collective_id=0, has_side_effects=True),
    )(*args)


def solution(mesh):
    in_specs = (
        P("seq", None),
        P(None, "head"),
        P("seq", None),
        P("seq", None),
        P("seq", None),
        P("seq", None),
        P("head", "seq"),
        P("head", "seq"),
        P("head"),
        P("seq", "head"),
    )
    out_specs = (
        P("seq", "head"),
        P("seq", "head"),
        P("seq", None),
        P("seq", None),
        P("seq", None),
        P("seq", None),
        P("head", "seq"),
        P("head", "seq"),
    )
    return jax.shard_map(local, mesh=mesh, in_specs=in_specs, out_specs=out_specs, check_vma=False)
```

```python
import functools
import math

import jax
import jax.numpy as jnp
from jax import lax
from jax.experimental import pallas as pl
from jax.experimental.pallas import tpu as pltpu
from jax.sharding import PartitionSpec as P

HIGH = lax.Precision.HIGHEST
BF = jnp.bfloat16
F32 = jnp.float32
Y = 8
C = 2
G = Y * C
MESH = pl.DeviceIdType.MESH


def greet(peers):
    barrier = pltpu.get_barrier_semaphore()
    for axis, first, count, step, me in peers:

        def signal(k, carry):
            peer = first + lax.rem(me + k, count) * step
            pl.semaphore_signal(barrier, inc=1, device_id={axis: peer}, device_id_type=MESH)
            return carry

        lax.fori_loop(1, count, signal, 0)


def greeted(peers):
    pl.semaphore_wait(pltpu.get_barrier_semaphore(), sum(p[2] - 1 for p in peers))


def spread_out(group, source, target, send_sem, recv_sem):
    axis, first, count, step, me = group
    pltpu.make_async_copy(source(me), target(me), recv_sem).start()

    def send(k, carry):
        peer = lax.rem(me + k, count)
        pltpu.make_async_remote_copy(
            src_ref=source(peer),
            dst_ref=target(me),
            send_sem=send_sem,
            recv_sem=recv_sem,
            device_id={axis: first + peer * step},
            device_id_type=MESH,
        ).start()
        return carry

    lax.fori_loop(1, count, send, 0)


def take(ref, sem):
    pltpu.make_async_copy(ref, ref, sem).wait()


NN = (((1,), (0,)), ((), ()))
NT = (((1,), (1,)), ((), ()))
TN = (((0,), (0,)), ((), ()))
UPS = ((True, False), (False, True))


def dot(a, b, dims, precision=None):
    return lax.dot_general(a, b, dims, precision=precision, preferred_element_type=F32)


def iota(shape, axis):
    return lax.broadcasted_iota(jnp.int32, shape, axis)


def layer_kernel(
    zs, heads, scale,
    x_ref, w_ref, ba_ref, ca_ref, bz_ref, cz_ref, da_ref, dz_ref, skip_ref, g_ref,
    gf_ref, gw_ref, gba_ref, gca_ref, gbz_ref, gcz_ref, gda_ref, gdz_ref,
    d8, sent, held, gains, total, tgain, zheld, zgains, back, states, ds,
    w_all, w_core, w_mid, w_one, w_low, w_two, m_own, m_all, f_own, f_all, sems,
):
    seq = lax.axis_index("seq")
    hd = lax.axis_index("head")
    z, r = seq // G, lax.rem(seq, G)
    y, core = r // C, lax.rem(r, C)
    groups = f_all.shape[0]
    near = ("seq", z * G, G, 1, r)
    far = ("seq", r, zs, G, z)
    along_c = ("seq", z * G + y * C, C, 1, core)
    along_y = ("seq", z * G + core, Y, C, y)
    along_x = ("head", 0, groups, 1, hd)
    greet([near, far, along_x])

    frames, wide = g_ref.shape
    size = wide // heads
    n = ba_ref.shape[1]
    rows = wide // G
    low_mask = iota((frames, frames), 1) <= iota((frames, frames), 0)
    high_mask = iota((frames, frames), 1) >= iota((frames, frames), 0)
    low_f, high_f = low_mask.astype(F32), high_mask.astype(F32)
    which = iota((2 * heads, wide), 1) // size
    pick = [(iota((2 * heads, wide), 0) - i * heads == which).astype(F32) for i in range(2)]
    d8[0:heads, :] = da_ref[...]
    d8[heads : 2 * heads, :] = dz_ref[...]
    d = d8[...]
    tgain[0] = jnp.broadcast_to(jnp.sum(d, axis=1, keepdims=True), (2 * heads, n))
    k_row = [dot(d, low_f, NT, HIGH), dot(d, high_f, NT, HIGH)]
    k_all = [dot(k_row[i], pick[i], TN, HIGH) for i in range(2)]
    edge = [k_all[0][frames - 1 : frames], k_all[1][0:1]]
    weight = [jnp.exp(edge[i] - k_all[i]) for i in range(2)]
    growth = [jnp.exp(k_all[i]) for i in range(2)]
    g = g_ref[...]
    g32 = g.astype(F32)
    maps_b = [ba_ref, bz_ref]
    maps_c = [ca_ref, cz_ref]
    x = dot(x_ref[...], w_ref[...], NN).astype(BF)
    x32 = x.astype(F32)
    weighted = [(x32 * weight[i]).astype(BF) for i in range(2)]
    greeted([near, far, along_x])
    spread_out(near, lambda k: tgain.at[0], lambda k: gains.at[k], sems.at[0], sems.at[1])
    for i in range(2):
        fresh = dot(weighted[i], maps_b[i][...], TN).astype(BF)
        query = dot(g32 * growth[i], maps_c[i][...].astype(F32), TN, HIGH).astype(BF)
        sent[i, :, 0] = fresh.reshape(G, rows, n)
        sent[i, :, 1] = query.reshape(G, rows, n)
        spread_out(
            near, lambda k: sent.at[i, k], lambda k: held.at[i, k], sems.at[2 + i], sems.at[4 + i]
        )

    lane_head = iota((frames, wide), 1) // size
    grad_x = jnp.zeros((frames, wide), F32)
    dk = jnp.zeros((2 * heads, frames), F32)
    daff = [None, None]
    for i in range(2):
        mask = low_mask if i == 0 else high_mask
        aff = dot(maps_c[i][...], maps_b[i][...], NT)
        pull = jnp.zeros((frames, frames), F32)
        for h in range(heads):
            gm = jnp.where(lane_head == h, g32, 0.0).astype(BF)
            if i == 0:
                ds[h] = dot(gm, x, NT).astype(BF)
            dscores = ds[h].astype(F32)
            row = i * heads + h
            kc = k_all[i][:, h * size : h * size + 1]
            kr = k_row[i][row : row + 1]
            decays = jnp.where(mask, jnp.exp(jnp.where(mask, kc - kr, 0.0)), 0.0)
            scores = decays * aff
            grad_x = grad_x + dot(scores.astype(BF), gm, TN)
            pull = pull + dscores * decays
            e = dscores * scores
            mine = iota((2 * heads, frames), 0) == row
            dk = dk + dot(mine.astype(F32), e, NT, HIGH)
            dk = dk - jnp.where(mine, jnp.sum(e, axis=0, keepdims=True), 0.0)
        daff[i] = pull.astype(BF)
        if i == 0:
            take(gains, sems.at[1])
            head = r // (G // heads)

            def grow(ref, j, side):
                return jnp.exp(ref[j, pl.ds(side * heads + head, 1), :])

            whole = gains[0]
            for j in range(1, G):
                whole = whole + gains[j]
            tgain[1] = whole
            spread_out(far, lambda k: tgain.at[1], lambda k: zgains.at[k], sems.at[6], sems.at[7])
            for side in range(2):
                take(held.at[side], sems.at[4 + side])
                for j0, up in enumerate(UPS[side]):
                    state = jnp.zeros((rows, n), F32)
                    for j in range(G) if up else range(G - 1, -1, -1):
                        state = grow(gains, j, side) * state + held[side, j, j0].astype(F32)
                    total[side, j0] = state
                spread_out(
                    far,
                    lambda k: total.at[side],
                    lambda k: zheld.at[side, k],
                    sems.at[8 + side],
                    sems.at[10 + side],
                )

    take(zgains, sems.at[7])
    for side in range(2):
        take(zheld.at[side], sems.at[10 + side])
        for j0, up in enumerate(UPS[side]):
            state = jnp.zeros((rows, n), F32)
            for j in range(zs) if up else range(zs - 1, -1, -1):
                new = grow(zgains, j, side) * state + zheld[side, j, j0]
                state = jnp.where((j < z) if up else (j > z), new, state)
            for j in range(G) if up else range(G - 1, -1, -1):
                back[side, j, j0] = state
                state = grow(gains, j, side) * state + held[side, j, j0].astype(F32)
        spread_out(
            near,
            lambda k: back.at[side, k],
            lambda k: states.at[side, k],
            sems.at[12 + side],
            sems.at[14 + side],
        )
    grad_b = [dot(daff[i], maps_c[i][...], TN) for i in range(2)]
    grad_c = [dot(daff[i], maps_b[i][...], NN) for i in range(2)]
    lane = iota((1, wide), 1) // size
    skip = jnp.zeros((1, wide), F32)
    for h in range(heads):
        skip = jnp.where(lane == h, skip_ref[h], skip)
    grad_x = grad_x + skip * g32

    last = jnp.zeros((2 * heads, n), F32)
    for i in range(2):
        take(states.at[i], sems.at[14 + i])
        s_in = states[i, :, 0].reshape(wide, n)
        g_out = states[i, :, 1].reshape(wide, n)
        g_low = g_out.astype(BF)
        scaled = dot(maps_b[i][...], g_low, NT) * weight[i]
        grad_x = grad_x + scaled
        u = dot(pick[i], scaled * x32, NT, HIGH)
        carried = dot(maps_c[i][...].astype(F32), s_in, NT, HIGH) * growth[i] * g32
        dk = dk - u + dot(pick[i], carried, NT, HIGH)
        both = dot(pick[i], g_out * s_in, NN, HIGH)
        fall = jnp.exp(jnp.sum(d, axis=1, keepdims=True))
        last = last + u + fall * both
        m_own[:, (2 * i) * n : (2 * i + 1) * n] = (grad_b[i] + dot(weighted[i], g_low, NN)).astype(BF)
        m_own[:, (2 * i + 1) * n : (2 * i + 2) * n] = (grad_c[i] + dot(g32 * growth[i], s_in, NN, HIGH)).astype(BF)
    gx = grad_x.astype(BF)
    piece = Y * C * w_all.shape[4]
    for k in range(zs):
        part = dot(x_ref[:, k * piece : (k + 1) * piece], gx, TN)
        for i in range(2):
            w_all[i, k] = part[:, i * n : (i + 1) * n].reshape(w_all.shape[2:]).astype(BF)
    for i in range(2):
        spread_out(
            along_c,
            lambda k: w_all.at[i, :, :, k],
            lambda k: w_core.at[i, k],
            sems.at[16 + i],
            sems.at[26 + i],
        )
    spread_out(along_x, lambda k: m_own, lambda k: m_all.at[k], sems.at[18], sems.at[19])
    for k in range(groups):
        f_own[k] = dot(gx, w_ref[k * wide : (k + 1) * wide, :], NT).astype(BF)
    spread_out(along_x, lambda k: f_own.at[k], lambda k: f_all.at[k], sems.at[20], sems.at[21])
    tri = jnp.where(iota((2 * heads, frames), 0) < heads, dot(dk, low_f, NN, HIGH), dot(dk, high_f, NN, HIGH))
    grad_d = tri + jnp.sum(last, axis=1, keepdims=True)
    gda_ref[...] = grad_d[0:heads]
    gdz_ref[...] = grad_d[heads : 2 * heads]
    first, second = (along_y, far), (far, along_y)
    for i in range(2):
        take(w_core.at[i], sems.at[26 + i])
        for j in range(Y):
            if i == 0:
                w_mid[i, j] = (w_core[i, 0, :, j].astype(F32) + w_core[i, 1, :, j].astype(F32)).astype(BF)
            else:
                w_mid[i, j] = (w_core[i, 0, j].astype(F32) + w_core[i, 1, j].astype(F32)).astype(BF)
        spread_out(
            first[i],
            lambda k: w_mid.at[i, k],
            lambda k: w_one.at[i, k],
            sems.at[22 + i],
            sems.at[28 + i],
        )
    for i in range(2):
        take(w_one.at[i], sems.at[28 + i])
        for k in range(Y):
            low = w_one[i, 0, k].astype(F32)
            for j in range(1, Y):
                low = low + w_one[i, j, k].astype(F32)
            w_low[i, k] = low.astype(BF)
        spread_out(
            second[i],
            lambda k: w_low.at[i, k],
            lambda k: w_two.at[i, k],
            sems.at[24 + i],
            sems.at[30 + i],
        )
    take(m_all, sems.at[19])
    for i, ref in enumerate((gba_ref, gca_ref, gbz_ref, gcz_ref)):
        m = m_all[0, :, i * n : (i + 1) * n].astype(F32)
        for j in range(1, groups):
            m = m + m_all[j, :, i * n : (i + 1) * n].astype(F32)
        ref[...] = m
    take(f_all, sems.at[21])
    f = f_all[0].astype(F32)
    for j in range(1, groups):
        f = f + f_all[j].astype(F32)
    gf_ref[...] = f.astype(BF)
    for i in range(2):
        take(w_two.at[i], sems.at[30 + i])
        low = w_two[i, 0].astype(F32)
        for j in range(1, Y):
            low = low + w_two[i, j].astype(F32)
        gw_ref[:, i * n : (i + 1) * n] = low * scale
    few, far_few, x_few = pl.ds(0, G - 1), pl.ds(0, zs - 1), pl.ds(0, groups - 1)
    take(gains.at[few], sems.at[0])
    take(zgains.at[far_few], sems.at[6])
    for i in range(2):
        take(held.at[i, few], sems.at[2 + i])
        take(zheld.at[i, far_few], sems.at[8 + i])
        take(back.at[i, few], sems.at[12 + i])
    take(m_all.at[x_few], sems.at[18])
    take(f_all.at[x_few], sems.at[20])
    for i in range(2):
        take(w_core.at[i, 0], sems.at[16 + i])
        take(w_one.at[i, far_few], sems.at[22 + i])
        take(w_two.at[i, far_few], sems.at[24 + i])


def hand_over(*refs):
    for source, target in zip(refs[:8], refs[8:]):
        target[...] = source[...]


def local(*args):
    features, w_in, b_a, _, _, _, decay_a, _, _, grad_y = args
    frames, deep = features.shape
    heads = decay_a.shape[0]
    wide = w_in.shape[1]
    n = b_a.shape[1]
    zs = lax.axis_size("seq") // G
    groups = lax.axis_size("head")
    cut = deep // (zs * G)
    rows = wide // G
    vmem = pl.BlockSpec(memory_space=pltpu.VMEM)
    smem = pl.BlockSpec(memory_space=pltpu.SMEM)
    scale = 1.0 / math.sqrt(frames * zs * G)
    out = jax.ShapeDtypeStruct
    shapes = [
        out((frames, deep // groups), BF),
        out((cut, wide), F32),
        out((frames, n), F32),
        out((frames, n), F32),
        out((frames, n), F32),
        out((frames, n), F32),
        out((heads, frames), F32),
        out((heads, frames), F32),
    ]
    results = pl.pallas_call(
        functools.partial(layer_kernel, zs, heads, scale),
        out_shape=shapes,
        in_specs=[vmem] * 8 + [smem, vmem],
        out_specs=[vmem] * 8,
        scratch_shapes=[
            pltpu.VMEM((2 * heads, frames), F32),
            pltpu.VMEM((2, G, 2, rows, n), BF),
            pltpu.VMEM((2, G, 2, rows, n), BF),
            pltpu.VMEM((G, 2 * heads, n), F32),
            pltpu.VMEM((2, 2, rows, n), F32),
            pltpu.VMEM((2, 2 * heads, n), F32),
            pltpu.VMEM((2, zs, 2, rows, n), F32),
            pltpu.VMEM((zs, 2 * heads, n), F32),
            pltpu.VMEM((2, G, 2, rows, n), F32),
            pltpu.VMEM((2, G, 2, rows, n), F32),
            pltpu.VMEM((heads, frames, frames), BF),
            pltpu.VMEM((2, zs, Y, C, cut, wide // 2), BF),
            pltpu.VMEM((2, C, zs, Y, cut, wide // 2), BF),
            pltpu.VMEM((2, Y, zs, cut, wide // 2), BF),
            pltpu.VMEM((2, Y, zs, cut, wide // 2), BF),
            pltpu.VMEM((2, zs, cut, wide // 2), BF),
            pltpu.VMEM((2, zs, cut, wide // 2), BF),
            pltpu.VMEM((frames, 4 * n), BF),
            pltpu.VMEM((groups, frames, 4 * n), BF),
            pltpu.VMEM((groups, frames, wide), BF),
            pltpu.VMEM((groups, frames, wide), BF),
            pltpu.SemaphoreType.DMA((32,)),
        ],
        compiler_params=pltpu.CompilerParams(collective_id=0, has_side_effects=True),
    )(*args)
    return pl.pallas_call(
        hand_over, out_shape=shapes, in_specs=[vmem] * 8, out_specs=[vmem] * 8
    )(*results)


def solution(mesh):
    in_specs = (
        P("seq", None),
        P(None, "head"),
        P("seq", None),
        P("seq", None),
        P("seq", None),
        P("seq", None),
        P("head", "seq"),
        P("head", "seq"),
        P("head"),
        P("seq", "head"),
    )
    out_specs = (
        P("seq", "head"),
        P("seq", "head"),
        P("seq", None),
        P("seq", None),
        P("seq", None),
        P("seq", None),
        P("head", "seq"),
        P("head", "seq"),
    )
    return jax.shard_map(local, mesh=mesh, in_specs=in_specs, out_specs=out_specs, check_vma=False)
```
